32 devices in a mesh: vec: 4 (over x, core), lat: 8 (over z, y).
Axes of the slice: x: 2, y: 2, z: 4, core: 2. Of those that a mesh axis runs over, the one named last changes fastest.
Arguments:
- perturbation: float32 [32, 3, 64, 2048], P('vec', None, 'lat'), may hold values from -6 to 6
- wind_coriolis: float32 [4, 3, 64, 2048], P(None, None, 'lat', 'vec'), may hold values from -4 to 4
- depth_field: float32 [4, 64, 2048], P(None, 'lat', 'vec'), may hold values from 0.5 to 2
Outputs:
- evolved: float32 [32, 3, 64, 2048], P('vec', None, 'lat')
The draws below stay inside these ranges and needn't reach their ends.
All inputs are finite; a program needn't handle non-finite values.
Results may differ from the reference program's by a relative error of at most 0.00002.
Values sent between devices are 32-bit elements; how exact they have to be, the bound alone decides.
A program may use at most 64 MiB of HBM per device.

```python
import math
import jax
import jax.numpy as jnp
from jax import lax

NLON = 2048
STEPS = 4
VECTORS = 32
NLAT = 64


def steps_of(rng, extent, split, smallest, top_value):
    def one(dim, blocks):
        steps = jax.random.uniform(jax.random.fold_in(jax.random.fold_in(rng, 6), dim), (blocks,), jnp.float32, smallest / len(split), top_value / len(split))
        return jnp.repeat(jnp.exp(steps), extent[dim] // blocks).reshape((-1,) + (1,) * (len(extent) - dim - 1))

    loudness = one(*split[0])
    for cut in split[1:]:
        loudness = loudness * one(*cut)
    return loudness


def scatter_about(key, extent, width, most, split=(), kind=jnp.bfloat16):
    values = jax.random.normal(key, extent, jnp.float32) * width
    if len(split) > 0:
        values = steps_of(key, extent, split, -0.22, 0.18) * values
    return jnp.clip(values, min=-most, max=most).astype(kind)


def setup_inputs(seed: int = 0) -> dict:
    streams_of = jax.random.split(jax.random.key(seed), 4)
    return {
        "perturbation": scatter_about(streams_of[0], (VECTORS, 3, NLAT, NLON), 1.0, 6.0, ((0, 4), (2, 8)), jnp.float32),
        "wind_coriolis": scatter_about(streams_of[1], (STEPS, 3, NLAT, NLON), 1.0, 4.0, ((2, 8), (3, 4)), jnp.float32),
        "depth_field": jnp.clip(jnp.exp(math.log(2.0) - 1.3862944 * jax.random.uniform(streams_of[2], (STEPS, NLAT, NLON), jnp.float32) ** steps_of(streams_of[2], (STEPS, NLAT, NLON), ((1, 8), (2, 4)), -0.2, 0.2)), 0.5, 2.0),
    }


time_step = 0.2
viscosity = 0.05


def lon_diff(field):
    return 0.5 * (jnp.roll(field, -1, axis=-1) - jnp.roll(field, 1, axis=-1))


def lat_diff(padded):
    return 0.5 * (padded[..., 2:, :] - padded[..., :-2, :])


def smooth(padded, centre):
    return padded[..., 2:, :] + padded[..., :-2, :] + jnp.roll(centre, -1, axis=-1) + jnp.roll(centre, 1, axis=-1) - 4.0 * centre


def advance(padded, coefficients):
    height_pad = padded[..., 0, :, :]
    zonal_pad = padded[..., 1, :, :]
    north_pad = padded[..., 2, :, :]
    height = height_pad[..., 1:-1, :]
    zonal = zonal_pad[..., 1:-1, :]
    north = north_pad[..., 1:-1, :]
    east_wind = coefficients[0]
    north_wind = coefficients[1]
    rotation = coefficients[2]
    depth_now = coefficients[3]
    tend_height = -(east_wind * lon_diff(height) + north_wind * lat_diff(height_pad) + depth_now * (lon_diff(zonal) + lat_diff(north_pad)))
    tend_zonal = -(east_wind * lon_diff(zonal) + north_wind * lat_diff(zonal_pad)) + rotation * north - lon_diff(height)
    tend_north = -(east_wind * lon_diff(north) + north_wind * lat_diff(north_pad)) - rotation * zonal - lat_diff(height_pad)
    new_height = height + time_step * (tend_height + viscosity * smooth(height_pad, height))
    new_zonal = zonal + time_step * (tend_zonal + viscosity * smooth(zonal_pad, zonal))
    new_north = north + time_step * (tend_north + viscosity * smooth(north_pad, north))
    return jnp.stack([new_height, new_zonal, new_north], axis=-3)


def reference(perturbation, wind_coriolis, depth_field):
    coefficients = jnp.concatenate([wind_coriolis, depth_field[:, None]], axis=1)

    def single(state):
        for moment in range(STEPS):
            padded = jnp.pad(state, ((0, 0), (1, 1), (0, 0)))
            state = advance(padded, coefficients[moment])
        return state

    return lax.map(single, perturbation)
```

```python
import functools

import jax
import jax.numpy as jnp
from jax import lax
from jax.experimental import pallas as pl
from jax.experimental.pallas import tpu as pltpu
from jax.sharding import PartitionSpec as P

MESH = pl.DeviceIdType.MESH
LANES = 128
LEAD = 3
time_step = 0.2
viscosity = 0.05
side_weight = time_step * viscosity
half_step = 0.5 * time_step


def sweep(load, store, halo, coefficient, tiles):
    lane = lax.broadcasted_iota(jnp.int32, (8, LANES), 1)
    row = lax.broadcasted_iota(jnp.int32, (8, LANES), 0)
    first_lane, last_lane = lane == 0, lane == LANES - 1
    first_row, last_row = row == 0, row == 7
    known = {}

    def tile(field, t):
        key = (field, t % tiles)
        if key not in known:
            value = load(field, t % tiles)
            known[key] = (value, pltpu.roll(value, LANES - 1, 1), pltpu.roll(value, 1, 1))
        return known[key]

    for t in range(tiles):
        east, west, rise, fall, here = {}, {}, {}, {}, {}
        for f in range(3):
            before, now, after = (tile(f, t + k) for k in (-1, 0, 1))
            here[f] = now[0]
            east[f] = jnp.where(last_lane, after[1], now[1])
            west[f] = jnp.where(first_lane, before[2], now[2])
            rise[f] = jnp.where(last_row, halo(1, f, t), pltpu.roll(now[0], 7, 0))
            fall[f] = jnp.where(first_row, halo(0, f, t), pltpu.roll(now[0], 1, 0))
        to_east, to_west, to_rise, to_fall, d, c = (coefficient(q, t) for q in range(6))
        new = [
            (1.0 - 4.0 * side_weight) * here[f]
            + (to_east * east[f] + to_west * west[f])
            + (to_rise * rise[f] + to_fall * fall[f])
            for f in range(3)
        ]
        new[0] -= c * ((east[1] - west[1]) + (rise[2] - fall[2]))
        new[1] += d * here[2] - half_step * (east[0] - west[0])
        new[2] -= d * here[1] + half_step * (rise[0] - fall[0])
        for f in range(3):
            store(f, t, new[f])


def kernel(
    nv, nl, x_hbm, wind, depth, out,
    ping, pong, leaving, halo, transit, own, table,
    x_sem, own_sem,
    gs, gr, hs, hr, ts, tr,
):
    count, _, rows, width = x_hbm.shape
    steps, part = wind.shape[0], wind.shape[3]
    tiles = width // LANES
    v, l = lax.axis_index("vec"), lax.axis_index("lat")
    has = (l > 0, l < nl - 1)
    other = (l - 1, l + 1)
    far = (l - 2, l + 2)
    reaches = (l > 1, l < nl - 2)
    pairs = nl // 2
    odd = lax.rem(l, 2)
    place = l // 2

    def share(number, wanted):
        return jnp.where(wanted, number * count // pairs, 0) if nl % 2 == 0 else jnp.int32(0)

    relayed = (
        share(place, (odd == 0) & reaches[0]),
        share(pairs - 1 - place, (odd == 1) & reaches[1]),
    )
    relaying = (
        share(place, (odd == 1) & reaches[0]),
        share(pairs - 1 - place, (odd == 0) & reaches[1]),
    )

    def turn(number, s, k):
        if s == steps - 1:
            return k < number
        return lax.rem(k * (count - number), count) >= count - number

    peers = [lax.rem(v + k, nv) for k in range(1, nv)]
    edge = (0, rows - 1)

    local = [
        pltpu.make_async_copy(wind, own.at[v, :, pl.ds(0, 3)], own_sem.at[0]),
        pltpu.make_async_copy(depth, own.at[v, :, 3], own_sem.at[1]),
        pltpu.make_async_copy(x_hbm, ping, x_sem.at[0]),
    ]
    for copy in local:
        copy.start()

    barrier = pltpu.get_barrier_semaphore()
    for peer in peers:
        pl.semaphore_signal(barrier, inc=1, device_id={"vec": peer}, device_id_type=MESH)
    for side in range(2):
        @pl.when(has[side])
        def _(side=side):
            pl.semaphore_signal(barrier, inc=1, device_id={"lat": other[side]}, device_id_type=MESH)
        @pl.when(reaches[side])
        def _(side=side):
            pl.semaphore_signal(barrier, inc=1, device_id={"lat": far[side]}, device_id_type=MESH)
    pl.semaphore_wait(barrier, nv - 1 + sum(flag.astype(jnp.int32) for flag in has + reaches))

    def remote(src, dst, send, recv, target):
        return pltpu.make_async_remote_copy(
            src_ref=src, dst_ref=dst, send_sem=send, recv_sem=recv,
            device_id=target, device_id_type=MESH,
        )

    def lap(s):
        return lax.rem(s, 2)

    def source(side, s, k):
        return x_hbm.at[k, :, pl.ds(edge[side], 1), :] if s == 0 else leaving.at[side, s - 1, k]

    def direct(side, s, k):
        return remote(
            source(side, s, k), halo.at[side, s, k],
            hs.at[side], hr.at[side, lap(s), k], {"lat": other[side]})

    def detour(side, s, k):
        return remote(
            source(side, s, k), transit.at[s, k],
            hs.at[side], tr.at[lap(s), k], {"lat": other[1 - side]})

    def arrival(side, s, k):
        at = transit.at[s, k]
        return remote(at, at, hs.at[side], tr.at[lap(s), k], {"lat": other[1 - side]})

    def onward(side, s, k):
        return remote(
            transit.at[s, k], halo.at[side, s, k],
            ts.at[0], hr.at[side, lap(s), k], {"lat": far[side]})

    def send(s, k):
        for side in range(2):
            @pl.when(turn(relayed[side], s, k))
            def _(side=side):
                detour(side, s, k).start()
        for side in range(2):
            @pl.when(has[side] & jnp.logical_not(turn(relayed[side], s, k)))
            def _(side=side):
                direct(side, s, k).start()

    def relay(s, k, due=None):
        for side in range(2):
            @pl.when(turn(relaying[side], s, k) if due is None else due[side])
            def _(side=side):
                arrival(side, s, k).wait_recv()
                onward(side, s, k).start()

    def sent():
        for side in range(2):
            @pl.when(has[side])
            def _(side=side):
                whole = halo.at[side, pl.ds(0, steps)]
                remote(whole, whole, hs.at[side], hr.at[side, 0, 0], {"lat": other[side]}).wait_send()
            for number in range(1, count + 1):
                @pl.when(relaying[side] == number)
                def _(side=side, number=number):
                    whole = transit.at[:, pl.ds(0, number)]
                    remote(whole, whole, ts.at[0], tr.at[0, 0], {"lat": far[side]}).wait_send()

    def spread(s, n, peer):
        return [
            remote(wind.at[s], own.at[v, s, pl.ds(0, 3)], gs.at[n], gr.at[s], {"vec": peer}),
            remote(depth.at[s], own.at[v, s, 3], gs.at[n], gr.at[s], {"vec": peer}),
        ]

    def gathered(s):
        whole = own.at[pl.ds(0, nv - 1), s]
        return remote(whole, whole, gs.at[0], gr.at[s], {"vec": peers[0]})

    send(0, 0)
    for n, peer in enumerate(peers):
        for copy in spread(0, n, peer):
            copy.start()

    @pl.loop(1, count)
    def _(k):
        send(0, k)

    for s in range(1, steps):
        for n, peer in enumerate(peers):
            for copy in spread(s, n, peer):
                copy.start()

    for side in range(2):
        @pl.when(jnp.logical_not(has[side]))
        def _(side=side):
            halo[1 - side, steps, 0] = jnp.zeros((3, 1, width), jnp.float32)

    for k in range(LEAD):
        relay(0, k)
    for copy in local:
        copy.wait()

    def span(t):
        return pl.ds(t * LANES, LANES)

    for s in range(steps):
        gathered(s).wait_recv()
        for t in range(tiles):
            block, offset = divmod(t * LANES, part)
            a, b, d, c = (own[block, s, q, :, pl.ds(offset, LANES)] for q in range(4))
            a, b = half_step * a, half_step * b
            values = (side_weight - a, side_weight + a, side_weight - b, side_weight + b, time_step * d, half_step * c)
            for q, value in enumerate(values):
                table[q, :, span(t)] = value

        final = s == steps - 1
        old = (ping, pong)[s % 2]
        new = out if final else (ping, pong)[(s + 1) % 2]

        @pl.loop(0, count)
        def _(k, s=s, final=final, old=old, new=new):
            ahead = k + LEAD
            later = ahead >= count
            due = []
            for side in range(2):
                now = turn(relaying[side], s, ahead) & jnp.logical_not(later)
                if not final:
                    now |= turn(relaying[side], s + 1, ahead - count) & later
                due.append(now)
            relay(s + later.astype(jnp.int32), jnp.where(later, ahead - count, ahead), due)
            for side in range(2):
                @pl.when(has[1 - side])
                def _(side=side):
                    direct(side, s, k).wait_recv()
            slot = [
                (jnp.where(has[side], s, steps), jnp.where(has[side], k, 0)) for side in range(2)
            ]

            def load(f, t):
                return old[k, f, :, span(t)]

            def store(f, t, value):
                new[k, f, :, span(t)] = value
                if not final:
                    for side in range(2):
                        leaving[side, s, k, f, :, span(t)] = value[edge[side]:edge[side] + 1]

            def beyond(side, f, t):
                value = halo[1 - side, slot[side][0], slot[side][1], f, :, span(t)]
                return jnp.broadcast_to(value, (rows, LANES))

            def coefficient(q, t):
                return table[q, :, span(t)]

            sweep(load, store, beyond, coefficient, tiles)
            if not final:
                send(s + 1, k)

    for n, peer in enumerate(peers):
        remote(own.at[v], own.at[v], gs.at[n], gr.at[0], {"vec": peer}).wait_send()
    sent()


def solution(mesh):
    nv, nl = mesh.shape["vec"], mesh.shape["lat"]

    def shards(perturbation, wind_coriolis, depth_field):
        count, _, rows, width = perturbation.shape
        steps, part = wind_coriolis.shape[0], wind_coriolis.shape[3]
        dma = pltpu.SemaphoreType.DMA
        f32 = jnp.float32
        return pl.pallas_call(
            functools.partial(kernel, nv, nl),
            out_shape=jax.ShapeDtypeStruct(perturbation.shape, f32),
            in_specs=[pl.BlockSpec(memory_space=pltpu.HBM)] * 3,
            out_specs=pl.BlockSpec(memory_space=pltpu.VMEM),
            scratch_shapes=[
                pltpu.VMEM((count, 3, rows, width), f32),
                pltpu.VMEM((count, 3, rows, width), f32),
                pltpu.VMEM((2, steps - 1, count, 3, 1, width), f32),
                pltpu.VMEM((2, steps + 1, count, 3, 1, width), f32),
                pltpu.VMEM((steps, count, 3, 1, width), f32),
                pltpu.VMEM((nv, steps, 4, rows, part), f32),
                pltpu.VMEM((6, rows, width), f32),
                dma((1,)), dma((2,)),
                dma((nv - 1,)), dma((steps,)), dma((2,)), dma((2, 2, count)), dma((1,)), dma((2, count)),
            ],
            compiler_params=pltpu.CompilerParams(
                collective_id=0, has_side_effects=True, vmem_limit_bytes=40 * 1024 * 1024
            ),
        )(*(pltpu.with_memory_space_constraint(a, pltpu.HBM) for a in (perturbation, wind_coriolis, depth_field)))

    placed = (P("vec", None, "lat", None), P(None, None, "lat", "vec"), P(None, "lat", "vec"))
    return jax.shard_map(
        shards, mesh=mesh, in_specs=placed, out_specs=P("vec", None, "lat", None), check_vma=False
    )
```

```python
import functools

import jax
import jax.numpy as jnp
from jax import lax
from jax.experimental import pallas as pl
from jax.experimental.pallas import tpu as pltpu
from jax.sharding import PartitionSpec as P

MESH = pl.DeviceIdType.MESH
LANES = 128
LEAD = 3
time_step = 0.2
viscosity = 0.05
side_weight = time_step * viscosity
half_step = 0.5 * time_step


def sweep(load, store, halo, coefficient, tiles):
    lane = lax.broadcasted_iota(jnp.int32, (8, LANES), 1)
    row = lax.broadcasted_iota(jnp.int32, (8, LANES), 0)
    first_lane, last_lane = lane == 0, lane == LANES - 1
    first_row, last_row = row == 0, row == 7
    known = {}

    def tile(field, t):
        key = (field, t % tiles)
        if key not in known:
            value = load(field, t % tiles)
            known[key] = (value, pltpu.roll(value, LANES - 1, 1), pltpu.roll(value, 1, 1))
        return known[key]

    for t in range(tiles):
        east, west, rise, fall, here = {}, {}, {}, {}, {}
        for f in range(3):
            before, now, after = (tile(f, t + k) for k in (-1, 0, 1))
            here[f] = now[0]
            east[f] = jnp.where(last_lane, after[1], now[1])
            west[f] = jnp.where(first_lane, before[2], now[2])
            rise[f] = jnp.where(last_row, halo(1, f, t), pltpu.roll(now[0], 7, 0))
            fall[f] = jnp.where(first_row, halo(0, f, t), pltpu.roll(now[0], 1, 0))
        to_east, to_west, to_rise, to_fall, d, c = (coefficient(q, t) for q in range(6))
        new = [
            (1.0 - 4.0 * side_weight) * here[f]
            + (to_east * east[f] + to_west * west[f])
            + (to_rise * rise[f] + to_fall * fall[f])
            for f in range(3)
        ]
        new[0] -= c * ((east[1] - west[1]) + (rise[2] - fall[2]))
        new[1] += d * here[2] - half_step * (east[0] - west[0])
        new[2] -= d * here[1] + half_step * (rise[0] - fall[0])
        for f in range(3):
            store(f, t, new[f])


def kernel(
    nv, nl, x_hbm, wind, depth, out,
    ping, pong, leaving, halo, transit, own, table,
    x_sem, own_sem,
    gs, gr, hs, hr, ts, tr,
):
    count, _, rows, width = x_hbm.shape
    steps, part = wind.shape[0], wind.shape[3]
    tiles = width // LANES
    v, l = lax.axis_index("vec"), lax.axis_index("lat")
    has = (l > 0, l < nl - 1)
    other = (l - 1, l + 1)
    far = (l - 2, l + 2)
    reaches = (l > 1, l < nl - 2)
    pairs = nl // 2
    odd = lax.rem(l, 2)
    place = l // 2

    def share(number, wanted):
        return jnp.where(wanted, number * count // pairs, 0) if nl % 2 == 0 else jnp.int32(0)

    relayed = (
        share(place, (odd == 0) & reaches[0]),
        share(pairs - 1 - place, (odd == 1) & reaches[1]),
    )
    relaying = (
        share(place, (odd == 1) & reaches[0]),
        share(pairs - 1 - place, (odd == 0) & reaches[1]),
    )

    def turn(number, s, k):
        if s == 0:
            return k >= count - number
        if s == steps - 1:
            return k < number // 2
        return lax.rem(k * (count - number), count) >= count - number

    peers = [lax.rem(v + k, nv) for k in range(1, nv)]
    edge = (0, rows - 1)

    local = [
        pltpu.make_async_copy(x_hbm, ping, x_sem.at[0]),
        pltpu.make_async_copy(wind, own.at[v, :, pl.ds(0, 3)], own_sem.at[0]),
        pltpu.make_async_copy(depth, own.at[v, :, 3], own_sem.at[1]),
    ]
    for copy in local:
        copy.start()

    barrier = pltpu.get_barrier_semaphore()
    for peer in peers:
        pl.semaphore_signal(barrier, inc=1, device_id={"vec": peer}, device_id_type=MESH)
    for side in range(2):
        @pl.when(has[side])
        def _(side=side):
            pl.semaphore_signal(barrier, inc=1, device_id={"lat": other[side]}, device_id_type=MESH)
        @pl.when(reaches[side])
        def _(side=side):
            pl.semaphore_signal(barrier, inc=1, device_id={"lat": far[side]}, device_id_type=MESH)
    pl.semaphore_wait(barrier, nv - 1 + sum(flag.astype(jnp.int32) for flag in has + reaches))

    def remote(src, dst, send, recv, target):
        return pltpu.make_async_remote_copy(
            src_ref=src, dst_ref=dst, send_sem=send, recv_sem=recv,
            device_id=target, device_id_type=MESH,
        )

    def lap(s):
        return lax.rem(s, 2)

    def source(side, s, k):
        return ping.at[k, :, pl.ds(edge[side], 1), :] if s == 0 else leaving.at[side, s - 1, k]

    def direct(side, s, k):
        return remote(
            source(side, s, k), halo.at[side, s, k],
            hs.at[side], hr.at[lap(s), k], {"lat": other[side]})

    def detour(side, s, k):
        return remote(
            source(side, s, k), transit.at[s * count + k],
            hs.at[side], tr.at[lap(s), k], {"lat": other[1 - side]})

    def arrival(side, s, k):
        at = transit.at[s * count + k]
        return remote(at, at, hs.at[side], tr.at[lap(s), k], {"lat": other[1 - side]})

    def onward(side, s, k):
        return remote(
            transit.at[s * count + k], halo.at[side, s, k],
            ts.at[0], hr.at[lap(s), k], {"lat": far[side]})

    def send(s, k):
        for side in range(2):
            @pl.when(turn(relayed[side], s, k))
            def _(side=side):
                detour(side, s, k).start()
        for side in range(2):
            @pl.when(has[side] & jnp.logical_not(turn(relayed[side], s, k)))
            def _(side=side):
                direct(side, s, k).start()

    def relay(s, k, due=None):
        for side in range(2):
            @pl.when(turn(relaying[side], s, k) if due is None else due[side])
            def _(side=side):
                arrival(side, s, k).wait_recv()
                onward(side, s, k).start()

    def sent():
        for side in range(2):
            @pl.when(has[side])
            def _(side=side):
                whole = halo.at[side, pl.ds(0, steps)]
                remote(whole, whole, hs.at[side], hr.at[0, 0], {"lat": other[side]}).wait_send()
            for number in range(1, count + 1):
                @pl.when(relaying[side] == number)
                def _(side=side, number=number):
                    whole = transit.at[pl.ds(0, (steps - 1) * number + number // 2)]
                    remote(whole, whole, ts.at[0], tr.at[0, 0], {"lat": far[side]}).wait_send()

    def spread(s, n, peer):
        return [
            remote(wind.at[s], own.at[v, s, pl.ds(0, 3)], gs.at[n], gr.at[s], {"vec": peer}),
            remote(depth.at[s], own.at[v, s, 3], gs.at[n], gr.at[s], {"vec": peer}),
        ]

    def gathered(s):
        whole = own.at[pl.ds(0, nv - 1), s]
        return remote(whole, whole, gs.at[0], gr.at[s], {"vec": peers[0]})

    local[0].wait()
    send(0, 0)
    for n, peer in enumerate(peers):
        for copy in spread(0, n, peer):
            copy.start()

    @pl.loop(1, count)
    def _(k):
        send(0, k)

    for s in range(1, steps):
        for n, peer in enumerate(peers):
            for copy in spread(s, n, peer):
                copy.start()

    for side in range(2):
        @pl.when(jnp.logical_not(has[side]))
        def _(side=side):
            halo[1 - side, steps, 0] = jnp.zeros((3, 1, width), jnp.float32)

    for k in range(LEAD):
        relay(0, k)
    for copy in local[1:]:
        copy.wait()

    def span(t):
        return pl.ds(t * LANES, LANES)

    for s in range(steps):
        gathered(s).wait_recv()
        for t in range(tiles):
            block, offset = divmod(t * LANES, part)
            a, b, d, c = (own[block, s, q, :, pl.ds(offset, LANES)] for q in range(4))
            a, b = half_step * a, half_step * b
            values = (side_weight - a, side_weight + a, side_weight - b, side_weight + b, time_step * d, half_step * c)
            for q, value in enumerate(values):
                table[q, :, span(t)] = value

        final = s == steps - 1
        old = ping if s == 0 else (out, pong)[s % 2]
        new = (pong, out)[s % 2]

        @pl.loop(0, count)
        def _(k, s=s, final=final, old=old, new=new):
            ahead = k + LEAD
            later = ahead >= count
            due = []
            for side in range(2):
                now = turn(relaying[side], s, ahead) & jnp.logical_not(later)
                if not final:
                    now |= turn(relaying[side], s + 1, ahead - count) & later
                due.append(now)
            relay(s + later.astype(jnp.int32), jnp.where(later, ahead - count, ahead), due)
            for ends in (1, 2):
                @pl.when(has[0].astype(jnp.int32) + has[1].astype(jnp.int32) == ends)
                def _(ends=ends):
                    both = halo.at[pl.ds(0, ends), s, k]
                    remote(both, both, hs.at[0], hr.at[lap(s), k], {"lat": other[0]}).wait_recv()
            slot = [
                (jnp.where(has[side], s, steps), jnp.where(has[side], k, 0)) for side in range(2)
            ]

            def load(f, t):
                return old[k, f, :, span(t)]

            def store(f, t, value):
                new[k, f, :, span(t)] = value
                if not final:
                    for side in range(2):
                        leaving[side, s, k, f, :, span(t)] = value[edge[side]:edge[side] + 1]

            def beyond(side, f, t):
                value = halo[1 - side, slot[side][0], slot[side][1], f, :, span(t)]
                return jnp.broadcast_to(value, (rows, LANES))

            def coefficient(q, t):
                return table[q, :, span(t)]

            sweep(load, store, beyond, coefficient, tiles)
            if not final:
                send(s + 1, k)

    for n, peer in enumerate(peers):
        remote(own.at[v], own.at[v], gs.at[n], gr.at[0], {"vec": peer}).wait_send()
    sent()


def solution(mesh):
    nv, nl = mesh.shape["vec"], mesh.shape["lat"]

    def shards(perturbation, wind_coriolis, depth_field):
        count, _, rows, width = perturbation.shape
        steps, part = wind_coriolis.shape[0], wind_coriolis.shape[3]
        dma = pltpu.SemaphoreType.DMA
        f32 = jnp.float32
        return pl.pallas_call(
            functools.partial(kernel, nv, nl),
            out_shape=jax.ShapeDtypeStruct(perturbation.shape, f32),
            in_specs=[pl.BlockSpec(memory_space=pltpu.HBM)] * 3,
            out_specs=pl.BlockSpec(memory_space=pltpu.VMEM),
            scratch_shapes=[
                pltpu.VMEM((count, 3, rows, width), f32),
                pltpu.VMEM((count, 3, rows, width), f32),
                pltpu.VMEM((2, steps - 1, count, 3, 1, width), f32),
                pltpu.VMEM((2, steps + 1, count, 3, 1, width), f32),
                pltpu.VMEM((steps * count, 3, 1, width), f32),
                pltpu.VMEM((nv, steps, 4, rows, part), f32),
                pltpu.VMEM((6, rows, width), f32),
                dma((1,)), dma((2,)),
                dma((nv - 1,)), dma((steps,)), dma((2,)), dma((2, count)), dma((1,)), dma((2, count)),
            ],
            compiler_params=pltpu.CompilerParams(
                collective_id=0, has_side_effects=True, vmem_limit_bytes=40 * 1024 * 1024
            ),
        )(*(pltpu.with_memory_space_constraint(a, pltpu.HBM) for a in (perturbation, wind_coriolis, depth_field)))

    placed = (P("vec", None, "lat", None), P(None, None, "lat", "vec"), P(None, "lat", "vec"))
    return jax.shard_map(
        shards, mesh=mesh, in_specs=placed, out_specs=P("vec", None, "lat", None), check_vma=False
    )
```

```python
import functools

import jax
import jax.numpy as jnp
from jax import lax
from jax.experimental import pallas as pl
from jax.experimental.pallas import tpu as pltpu
from jax.sharding import PartitionSpec as P

MESH = pl.DeviceIdType.MESH
LANES = 128
LEAD = 3
time_step = 0.2
viscosity = 0.05
side_weight = time_step * viscosity
half_step = 0.5 * time_step


def sweep(load, store, halo, coefficient, tiles):
    lane = lax.broadcasted_iota(jnp.int32, (8, LANES), 1)
    row = lax.broadcasted_iota(jnp.int32, (8, LANES), 0)
    first_lane, last_lane = lane == 0, lane == LANES - 1
    first_row, last_row = row == 0, row == 7
    known = {}

    def tile(field, t):
        key = (field, t % tiles)
        if key not in known:
            value = load(field, t % tiles)
            known[key] = (value, pltpu.roll(value, LANES - 1, 1), pltpu.roll(value, 1, 1))
        return known[key]

    for t in range(tiles):
        east, west, rise, fall, here = {}, {}, {}, {}, {}
        for f in range(3):
            before, now, after = (tile(f, t + k) for k in (-1, 0, 1))
            here[f] = now[0]
            east[f] = jnp.where(last_lane, after[1], now[1])
            west[f] = jnp.where(first_lane, before[2], now[2])
            rise[f] = jnp.where(last_row, halo(1, f, t), pltpu.roll(now[0], 7, 0))
            fall[f] = jnp.where(first_row, halo(0, f, t), pltpu.roll(now[0], 1, 0))
        to_east, to_west, to_rise, to_fall, d, c = (coefficient(q, t) for q in range(6))
        new = [
            (1.0 - 4.0 * side_weight) * here[f]
            + (to_east * east[f] + to_west * west[f])
            + (to_rise * rise[f] + to_fall * fall[f])
            for f in range(3)
        ]
        new[0] -= c * ((east[1] - west[1]) + (rise[2] - fall[2]))
        new[1] += d * here[2] - half_step * (east[0] - west[0])
        new[2] -= d * here[1] + half_step * (rise[0] - fall[0])
        for f in range(3):
            store(f, t, new[f])


def kernel(
    nv, nl, x_hbm, wind, depth, out,
    ping, pong, leaving, halo, transit, own, table,
    x_sem, own_sem,
    gs, gr, hs, hr, ts, tr, below, beside, across,
):
    count, _, rows, width = x_hbm.shape
    steps, part = wind.shape[0], wind.shape[3]
    tiles = width // LANES
    v, l = lax.axis_index("vec"), lax.axis_index("lat")
    has = (l > 0, l < nl - 1)
    other = (l - 1, l + 1)
    far = (l - 2, l + 2)
    reaches = (l > 1, l < nl - 2)
    pairs = nl // 2
    odd = lax.rem(l, 2)
    place = l // 2

    def share(number, wanted):
        return jnp.where(wanted, number * count // pairs, 0) if nl % 2 == 0 else jnp.int32(0)

    relayed = (
        share(place, (odd == 0) & reaches[0]),
        share(pairs - 1 - place, (odd == 1) & reaches[1]),
    )
    relaying = (
        share(place, (odd == 1) & reaches[0]),
        share(pairs - 1 - place, (odd == 0) & reaches[1]),
    )

    def turn(number, s, k):
        if s == 0:
            return k >= count - number
        if s == steps - 1:
            return k < number // 2
        return lax.rem(k * (count - number), count) >= count - number

    peers = [lax.rem(v + k, nv) for k in range(1, nv)]
    edge = (0, rows - 1)

    local = [
        pltpu.make_async_copy(x_hbm, ping, x_sem.at[0]),
        pltpu.make_async_copy(wind, own.at[v, :, pl.ds(0, 3)], own_sem.at[0]),
        pltpu.make_async_copy(depth, own.at[v, :, 3], own_sem.at[1]),
    ]
    mate = l + 1 - 2 * odd

    barrier = pltpu.get_barrier_semaphore()

    def greet(semaphore, wanted, device):
        @pl.when(wanted)
        def _():
            pl.semaphore_signal(semaphore, inc=1, device_id=device, device_id_type=MESH)

    pl.semaphore_signal(barrier, inc=1, device_id={"lat": mate}, device_id_type=MESH)
    greet(barrier, reaches[1], {"lat": far[1]})
    for peer in peers:
        greet(barrier, peer > v, {"vec": peer})
    for copy in local:
        copy.start()
    pl.semaphore_wait(barrier, 1 + v + reaches[0].astype(jnp.int32))

    def remote(src, dst, send, recv, target):
        return pltpu.make_async_remote_copy(
            src_ref=src, dst_ref=dst, send_sem=send, recv_sem=recv,
            device_id=target, device_id_type=MESH,
        )

    def lap(s):
        return lax.rem(s, 2)

    def source(side, s, k):
        return ping.at[k, :, pl.ds(edge[side], 1), :] if s == 0 else leaving.at[side, s - 1, k]

    def direct(side, s, k):
        return remote(
            source(side, s, k), halo.at[side, s, k],
            hs.at[side], hr.at[lap(s), k], {"lat": other[side]})

    def detour(side, s, k):
        return remote(
            source(side, s, k), transit.at[s * count + k],
            hs.at[side], tr.at[lap(s), k], {"lat": other[1 - side]})

    def arrival(side, s, k):
        at = transit.at[s * count + k]
        return remote(at, at, hs.at[side], tr.at[lap(s), k], {"lat": other[1 - side]})

    def onward(side, s, k):
        return remote(
            transit.at[s * count + k], halo.at[side, s, k],
            ts.at[0], hr.at[lap(s), k], {"lat": far[side]})

    def send(s, k, which=(True, True)):
        for side in range(2):
            near = odd == 1 - side
            around = turn(relayed[side], s, k)
            if which[0]:
                @pl.when(around)
                def _(side=side):
                    detour(side, s, k).start()
        for side in range(2):
            near = odd == 1 - side
            around = turn(relayed[side], s, k)
            straight = has[side] & jnp.logical_not(around)
            if not which[0]:
                straight &= jnp.logical_not(near)
            if not which[1]:
                straight &= near
            @pl.when(straight)
            def _(side=side):
                direct(side, s, k).start()

    def relay(s, k, due=None):
        for side in range(2):
            @pl.when(turn(relaying[side], s, k) if due is None else due[side])
            def _(side=side):
                arrival(side, s, k).wait_recv()
                onward(side, s, k).start()

    def sent():
        for side in range(2):
            @pl.when(has[side])
            def _(side=side):
                whole = halo.at[side, pl.ds(0, steps)]
                remote(whole, whole, hs.at[side], hr.at[0, 0], {"lat": other[side]}).wait_send()
            for number in range(1, count + 1):
                @pl.when(relaying[side] == number)
                def _(side=side, number=number):
                    whole = transit.at[pl.ds(0, (steps - 1) * number + number // 2)]
                    remote(whole, whole, ts.at[0], tr.at[0, 0], {"lat": far[side]}).wait_send()

    def spread(s, n, peer):
        return [
            remote(wind.at[s], own.at[v, s, pl.ds(0, 3)], gs.at[0], gr.at[s], {"vec": peer}),
            remote(depth.at[s], own.at[v, s, 3], gs.at[0], gr.at[s], {"vec": peer}),
        ]

    def gathered(s):
        whole = own.at[pl.ds(0, nv - 1), s]
        return remote(whole, whole, gs.at[0], gr.at[s], {"vec": peers[0]})

    greet(below, reaches[0], {"lat": far[0]})
    greet(beside, (odd == 1) & reaches[0], {"lat": mate})
    for peer in peers:
        greet(across, peer < v, {"vec": peer})
    local[0].wait()

    @pl.loop(0, count)
    def _(k):
        send(0, k, (True, False))

    def share_out(s, wanted):
        for n, peer in enumerate(peers):
            @pl.when(wanted(peer))
            def _(s=s, n=n, peer=peer):
                for copy in spread(s, n, peer):
                    copy.start()

    share_out(0, lambda peer: peer < v)

    @pl.when((odd == 1) & reaches[1])
    def _():
        pl.semaphore_wait(below, 1)

    @pl.when((odd == 0) & reaches[0])
    def _():
        pl.semaphore_wait(beside, 1)

    @pl.loop(0, count)
    def _(k):
        send(0, k, (False, True))

    @pl.when(v < nv - 1)
    def _():
        pl.semaphore_wait(across, nv - 1 - v)

    share_out(0, lambda peer: peer > v)
    for s in range(1, steps):
        share_out(s, lambda peer: peer >= 0)

    @pl.when((odd == 0) & reaches[1])
    def _():
        pl.semaphore_wait(below, 1)

    for side in range(2):
        @pl.when(jnp.logical_not(has[side]))
        def _(side=side):
            halo[1 - side, steps, 0] = jnp.zeros((3, 1, width), jnp.float32)

    for k in range(LEAD):
        relay(0, k)
    for copy in local[1:]:
        copy.wait()

    def span(t):
        return pl.ds(t * LANES, LANES)

    for s in range(steps):
        gathered(s).wait_recv()
        for t in range(tiles):
            block, offset = divmod(t * LANES, part)
            a, b, d, c = (own[block, s, q, :, pl.ds(offset, LANES)] for q in range(4))
            a, b = half_step * a, half_step * b
            values = (side_weight - a, side_weight + a, side_weight - b, side_weight + b, time_step * d, half_step * c)
            for q, value in enumerate(values):
                table[q, :, span(t)] = value

        final = s == steps - 1
        old = ping if s == 0 else (out, pong)[(steps - s) % 2]
        new = (out, pong)[(steps - 1 - s) % 2]

        @pl.loop(0, count)
        def _(k, s=s, final=final, old=old, new=new):
            ahead = k + LEAD
            later = ahead >= count
            due = []
            for side in range(2):
                now = turn(relaying[side], s, ahead) & jnp.logical_not(later)
                if not final:
                    now |= turn(relaying[side], s + 1, ahead - count) & later
                due.append(now)
            relay(s + later.astype(jnp.int32), jnp.where(later, ahead - count, ahead), due)
            for ends in (1, 2):
                @pl.when(has[0].astype(jnp.int32) + has[1].astype(jnp.int32) == ends)
                def _(ends=ends):
                    both = halo.at[pl.ds(0, ends), s, k]
                    remote(both, both, hs.at[0], hr.at[lap(s), k], {"lat": other[0]}).wait_recv()
            slot = [
                (jnp.where(has[side], s, steps), jnp.where(has[side], k, 0)) for side in range(2)
            ]

            def load(f, t):
                return old[k, f, :, span(t)]

            def store(f, t, value):
                new[k, f, :, span(t)] = value
                if not final:
                    for side in range(2):
                        leaving[side, s, k, f, :, span(t)] = value[edge[side]:edge[side] + 1]

            def beyond(side, f, t):
                value = halo[1 - side, slot[side][0], slot[side][1], f, :, span(t)]
                return jnp.broadcast_to(value, (rows, LANES))

            def coefficient(q, t):
                return table[q, :, span(t)]

            sweep(load, store, beyond, coefficient, tiles)
            if not final:
                send(s + 1, k)

    whole = own.at[pl.ds(0, nv - 1)]
    remote(whole, whole, gs.at[0], gr.at[0], {"vec": peers[0]}).wait_send()
    sent()


def solution(mesh):
    nv, nl = mesh.shape["vec"], mesh.shape["lat"]

    def shards(perturbation, wind_coriolis, depth_field):
        count, _, rows, width = perturbation.shape
        steps, part = wind_coriolis.shape[0], wind_coriolis.shape[3]
        dma = pltpu.SemaphoreType.DMA
        f32 = jnp.float32
        return pl.pallas_call(
            functools.partial(kernel, nv, nl),
            out_shape=jax.ShapeDtypeStruct(perturbation.shape, f32),
            in_specs=[pl.BlockSpec(memory_space=pltpu.HBM)] * 3,
            out_specs=pl.BlockSpec(memory_space=pltpu.VMEM),
            scratch_shapes=[
                pltpu.VMEM((count, 3, rows, width), f32),
                pltpu.VMEM((count, 3, rows, width), f32),
                pltpu.VMEM((2, steps - 1, count, 3, 1, width), f32),
                pltpu.VMEM((2, steps + 1, count, 3, 1, width), f32),
                pltpu.VMEM((steps * count, 3, 1, width), f32),
                pltpu.VMEM((nv, steps, 4, rows, part), f32),
                pltpu.VMEM((6, rows, width), f32),
                dma((1,)), dma((2,)),
                dma((1,)), dma((steps,)), dma((2,)), dma((2, count)), dma((1,)), dma((2, count)),
                pltpu.SemaphoreType.REGULAR, pltpu.SemaphoreType.REGULAR, pltpu.SemaphoreType.REGULAR,
            ],
            compiler_params=pltpu.CompilerParams(
                collective_id=0, has_side_effects=True, vmem_limit_bytes=40 * 1024 * 1024
            ),
        )(*(pltpu.with_memory_space_constraint(a, pltpu.HBM) for a in (perturbation, wind_coriolis, depth_field)))

    placed = (P("vec", None, "lat", None), P(None, None, "lat", "vec"), P(None, "lat", "vec"))
    return jax.shard_map(
        shards, mesh=mesh, in_specs=placed, out_specs=P("vec", None, "lat", None), check_vma=False
    )
```

```python
import functools

import jax
import jax.numpy as jnp
from jax import lax
from jax.experimental import pallas as pl
from jax.experimental.pallas import tpu as pltpu
from jax.sharding import PartitionSpec as P

MESH = pl.DeviceIdType.MESH
LANES = 128
LEAD = 3
time_step = 0.2
viscosity = 0.05
side_weight = time_step * viscosity
half_step = 0.5 * time_step


def sweep(load, store, halo, coefficient, tiles):
    lane = lax.broadcasted_iota(jnp.int32, (8, LANES), 1)
    row = lax.broadcasted_iota(jnp.int32, (8, LANES), 0)
    first_lane, last_lane = lane == 0, lane == LANES - 1
    first_row, last_row = row == 0, row == 7
    known = {}

    def tile(field, t):
        key = (field, t % tiles)
        if key not in known:
            value = load(field, t % tiles)
            known[key] = (value, pltpu.roll(value, LANES - 1, 1), pltpu.roll(value, 1, 1))
        return known[key]

    for t in range(tiles):
        east, west, rise, fall, here = {}, {}, {}, {}, {}
        for f in range(3):
            before, now, after = (tile(f, t + k) for k in (-1, 0, 1))
            here[f] = now[0]
            east[f] = jnp.where(last_lane, after[1], now[1])
            west[f] = jnp.where(first_lane, before[2], now[2])
            rise[f] = jnp.where(last_row, halo(1, f, t), pltpu.roll(now[0], 7, 0))
            fall[f] = jnp.where(first_row, halo(0, f, t), pltpu.roll(now[0], 1, 0))
        to_east, to_west, to_rise, to_fall, d, c = (coefficient(q, t) for q in range(6))
        new = [
            (1.0 - 4.0 * side_weight) * here[f]
            + (to_east * east[f] + to_west * west[f])
            + (to_rise * rise[f] + to_fall * fall[f])
            for f in range(3)
        ]
        new[0] -= c * ((east[1] - west[1]) + (rise[2] - fall[2]))
        new[1] += d * here[2] - half_step * (east[0] - west[0])
        new[2] -= d * here[1] + half_step * (rise[0] - fall[0])
        for f in range(3):
            store(f, t, new[f])


def kernel(
    nv, nl, x_hbm, wind, depth, out,
    ping, pong, leaving, halo, transit, own, table,
    x_sem, own_sem,
    gs, gr, hs, hr, ts, tr, below, beside, across,
):
    count, _, rows, width = x_hbm.shape
    steps, part = wind.shape[0], wind.shape[3]
    tiles = width // LANES
    v, l = lax.axis_index("vec"), lax.axis_index("lat")
    has = (l > 0, l < nl - 1)
    other = (l - 1, l + 1)
    far = (l - 2, l + 2)
    reaches = (l > 1, l < nl - 2)
    pairs = nl // 2
    odd = lax.rem(l, 2)
    place = l // 2

    def share(number, wanted):
        return jnp.where(wanted, number * count // pairs, 0) if nl % 2 == 0 else jnp.int32(0)

    relayed = (
        share(place, (odd == 0) & reaches[0]),
        share(pairs - 1 - place, (odd == 1) & reaches[1]),
    )
    relaying = (
        share(place, (odd == 1) & reaches[0]),
        share(pairs - 1 - place, (odd == 0) & reaches[1]),
    )

    def turn(number, s, k):
        if s == 0:
            return k >= count - number
        if s == steps - 1:
            return k < number // 2
        return lax.rem(k * (count - number), count) >= count - number

    peers = [lax.rem(v + k, nv) for k in range(1, nv)]
    edge = (0, rows - 1)

    local = [
        pltpu.make_async_copy(x_hbm, ping, x_sem.at[0]),
        pltpu.make_async_copy(wind, own.at[v, :, pl.ds(0, 3)], own_sem.at[0]),
        pltpu.make_async_copy(depth, own.at[v, :, 3], own_sem.at[1]),
    ]
    mate = l + 1 - 2 * odd

    barrier = pltpu.get_barrier_semaphore()

    def greet(semaphore, wanted, device):
        @pl.when(wanted)
        def _():
            pl.semaphore_signal(semaphore, inc=1, device_id=device, device_id_type=MESH)

    pl.semaphore_signal(barrier, inc=1, device_id={"lat": mate}, device_id_type=MESH)
    greet(barrier, reaches[1], {"lat": far[1]})
    for peer in peers:
        greet(barrier, peer > v, {"vec": peer})
    for copy in local:
        copy.start()
    pl.semaphore_wait(barrier, 1 + v + reaches[0].astype(jnp.int32))

    def remote(src, dst, send, recv, target):
        return pltpu.make_async_remote_copy(
            src_ref=src, dst_ref=dst, send_sem=send, recv_sem=recv,
            device_id=target, device_id_type=MESH,
        )

    def lap(s):
        return lax.rem(s, 2)

    def source(side, s, k):
        return x_hbm.at[k, :, pl.ds(edge[side], 1), :] if s == 0 else leaving.at[side, s - 1, k]

    def direct(side, s, k):
        return remote(
            source(side, s, k), halo.at[side, s, k],
            hs.at[side], hr.at[lap(s), k], {"lat": other[side]})

    def detour(side, s, k):
        return remote(
            source(side, s, k), transit.at[s * count + k],
            hs.at[side], tr.at[lap(s), k], {"lat": other[1 - side]})

    def arrival(side, s, k):
        at = transit.at[s * count + k]
        return remote(at, at, hs.at[side], tr.at[lap(s), k], {"lat": other[1 - side]})

    def onward(side, s, k):
        return remote(
            transit.at[s * count + k], halo.at[side, s, k],
            ts.at[0], hr.at[lap(s), k], {"lat": far[side]})

    def send(s, k, which=(True, True)):
        for side in range(2):
            near = odd == 1 - side
            around = turn(relayed[side], s, k)
            if which[0]:
                @pl.when(around)
                def _(side=side):
                    detour(side, s, k).start()
        for side in range(2):
            near = odd == 1 - side
            around = turn(relayed[side], s, k)
            straight = has[side] & jnp.logical_not(around)
            if not which[0]:
                straight &= jnp.logical_not(near)
            if not which[1]:
                straight &= near
            @pl.when(straight)
            def _(side=side):
                direct(side, s, k).start()

    def relay(s, k, due=None):
        for side in range(2):
            @pl.when(turn(relaying[side], s, k) if due is None else due[side])
            def _(side=side):
                arrival(side, s, k).wait_recv()
                onward(side, s, k).start()

    def sent():
        for side in range(2):
            @pl.when(has[side])
            def _(side=side):
                whole = halo.at[side, pl.ds(0, steps)]
                remote(whole, whole, hs.at[side], hr.at[0, 0], {"lat": other[side]}).wait_send()
            for number in range(1, count + 1):
                @pl.when(relaying[side] == number)
                def _(side=side, number=number):
                    whole = transit.at[pl.ds(0, (steps - 1) * number + number // 2)]
                    remote(whole, whole, ts.at[0], tr.at[0, 0], {"lat": far[side]}).wait_send()

    def spread(s, n, peer):
        return [
            remote(wind.at[s], own.at[v, s, pl.ds(0, 3)], gs.at[0], gr.at[s], {"vec": peer}),
            remote(depth.at[s], own.at[v, s, 3], gs.at[0], gr.at[s], {"vec": peer}),
        ]

    def gathered(s):
        whole = own.at[pl.ds(0, nv - 1), s]
        return remote(whole, whole, gs.at[0], gr.at[s], {"vec": peers[0]})

    greet(below, reaches[0], {"lat": far[0]})
    greet(beside, (odd == 1) & reaches[0], {"lat": mate})
    for peer in peers:
        greet(across, peer < v, {"vec": peer})
    @pl.loop(0, count)
    def _(k):
        send(0, k, (True, False))

    def share_out(s, wanted):
        for n, peer in enumerate(peers):
            @pl.when(wanted(peer))
            def _(s=s, n=n, peer=peer):
                for copy in spread(s, n, peer):
                    copy.start()

    share_out(0, lambda peer: peer < v)

    @pl.when((odd == 1) & reaches[1])
    def _():
        pl.semaphore_wait(below, 1)

    @pl.when((odd == 0) & reaches[0])
    def _():
        pl.semaphore_wait(beside, 1)

    @pl.loop(0, count)
    def _(k):
        send(0, k, (False, True))

    @pl.when(v < nv - 1)
    def _():
        pl.semaphore_wait(across, nv - 1 - v)

    share_out(0, lambda peer: peer > v)
    for s in range(1, steps):
        share_out(s, lambda peer: peer >= 0)

    @pl.when((odd == 0) & reaches[1])
    def _():
        pl.semaphore_wait(below, 1)

    for side in range(2):
        @pl.when(jnp.logical_not(has[side]))
        def _(side=side):
            halo[1 - side, steps, 0] = jnp.zeros((3, 1, width), jnp.float32)

    for k in range(LEAD):
        relay(0, k)
    for copy in local:
        copy.wait()

    def span(t):
        return pl.ds(t * LANES, LANES)

    for s in range(steps):
        gathered(s).wait_recv()
        for t in range(tiles):
            block, offset = divmod(t * LANES, part)
            a, b, d, c = (own[block, s, q, :, pl.ds(offset, LANES)] for q in range(4))
            a, b = half_step * a, half_step * b
            values = (side_weight - a, side_weight + a, side_weight - b, side_weight + b, time_step * d, half_step * c)
            for q, value in enumerate(values):
                table[q, :, span(t)] = value

        final = s == steps - 1
        old = ping if s == 0 else (out, pong)[(steps - s) % 2]
        new = (out, pong)[(steps - 1 - s) % 2]

        @pl.loop(0, count)
        def _(k, s=s, final=final, old=old, new=new):
            ahead = k + LEAD
            later = ahead >= count
            due = []
            for side in range(2):
                now = turn(relaying[side], s, ahead) & jnp.logical_not(later)
                if not final:
                    now |= turn(relaying[side], s + 1, ahead - count) & later
                due.append(now)
            relay(s + later.astype(jnp.int32), jnp.where(later, ahead - count, ahead), due)
            for ends in (1, 2):
                @pl.when(has[0].astype(jnp.int32) + has[1].astype(jnp.int32) == ends)
                def _(ends=ends):
                    both = halo.at[pl.ds(0, ends), s, k]
                    remote(both, both, hs.at[0], hr.at[lap(s), k], {"lat": other[0]}).wait_recv()
            slot = [
                (jnp.where(has[side], s, steps), jnp.where(has[side], k, 0)) for side in range(2)
            ]

            def load(f, t):
                return old[k, f, :, span(t)]

            def store(f, t, value):
                new[k, f, :, span(t)] = value
                if not final:
                    for side in range(2):
                        leaving[side, s, k, f, :, span(t)] = value[edge[side]:edge[side] + 1]

            def beyond(side, f, t):
                value = halo[1 - side, slot[side][0], slot[side][1], f, :, span(t)]
                return jnp.broadcast_to(value, (rows, LANES))

            def coefficient(q, t):
                return table[q, :, span(t)]

            sweep(load, store, beyond, coefficient, tiles)
            if not final:
                send(s + 1, k)

    whole = own.at[pl.ds(0, nv - 1)]
    remote(whole, whole, gs.at[0], gr.at[0], {"vec": peers[0]}).wait_send()
    sent()


def solution(mesh):
    nv, nl = mesh.shape["vec"], mesh.shape["lat"]

    def shards(perturbation, wind_coriolis, depth_field):
        count, _, rows, width = perturbation.shape
        steps, part = wind_coriolis.shape[0], wind_coriolis.shape[3]
        dma = pltpu.SemaphoreType.DMA
        f32 = jnp.float32
        return pl.pallas_call(
            functools.partial(kernel, nv, nl),
            out_shape=jax.ShapeDtypeStruct(perturbation.shape, f32),
            in_specs=[pl.BlockSpec(memory_space=pltpu.HBM)] * 3,
            out_specs=pl.BlockSpec(memory_space=pltpu.VMEM),
            scratch_shapes=[
                pltpu.VMEM((count, 3, rows, width), f32),
                pltpu.VMEM((count, 3, rows, width), f32),
                pltpu.VMEM((2, steps - 1, count, 3, 1, width), f32),
                pltpu.VMEM((2, steps + 1, count, 3, 1, width), f32),
                pltpu.VMEM((steps * count, 3, 1, width), f32),
                pltpu.VMEM((nv, steps, 4, rows, part), f32),
                pltpu.VMEM((6, rows, width), f32),
                dma((1,)), dma((2,)),
                dma((1,)), dma((steps,)), dma((2,)), dma((2, count)), dma((1,)), dma((2, count)),
                pltpu.SemaphoreType.REGULAR, pltpu.SemaphoreType.REGULAR, pltpu.SemaphoreType.REGULAR,
            ],
            compiler_params=pltpu.CompilerParams(
                collective_id=0, has_side_effects=True, vmem_limit_bytes=40 * 1024 * 1024
            ),
        )(*(pltpu.with_memory_space_constraint(a, pltpu.HBM) for a in (perturbation, wind_coriolis, depth_field)))

    placed = (P("vec", None, "lat", None), P(None, None, "lat", "vec"), P(None, "lat", "vec"))
    return jax.shard_map(
        shards, mesh=mesh, in_specs=placed, out_specs=P("vec", None, "lat", None), check_vma=False
    )
```

```python
import functools

import jax
import jax.numpy as jnp
from jax import lax
from jax.experimental import pallas as pl
from jax.experimental.pallas import tpu as pltpu
from jax.sharding import PartitionSpec as P

MESH = pl.DeviceIdType.MESH
LANES = 128
LEAD = 3
time_step = 0.2
viscosity = 0.05
side_weight = time_step * viscosity
half_step = 0.5 * time_step


def sweep(load, store, halo, coefficient, tiles):
    lane = lax.broadcasted_iota(jnp.int32, (8, LANES), 1)
    row = lax.broadcasted_iota(jnp.int32, (8, LANES), 0)
    first_lane, last_lane = lane == 0, lane == LANES - 1
    first_row, last_row = row == 0, row == 7
    known = {}

    def tile(field, t):
        key = (field, t % tiles)
        if key not in known:
            value = load(field, t % tiles)
            known[key] = (value, pltpu.roll(value, LANES - 1, 1), pltpu.roll(value, 1, 1))
        return known[key]

    for t in range(tiles):
        east, west, rise, fall, here = {}, {}, {}, {}, {}
        for f in range(3):
            before, now, after = (tile(f, t + k) for k in (-1, 0, 1))
            here[f] = now[0]
            east[f] = jnp.where(last_lane, after[1], now[1])
            west[f] = jnp.where(first_lane, before[2], now[2])
            rise[f] = jnp.where(last_row, halo(1, f, t), pltpu.roll(now[0], 7, 0))
            fall[f] = jnp.where(first_row, halo(0, f, t), pltpu.roll(now[0], 1, 0))
        to_east, to_west, to_rise, to_fall, d, c = (coefficient(q, t) for q in range(6))
        new = [
            (1.0 - 4.0 * side_weight) * here[f]
            + (to_east * east[f] + to_west * west[f])
            + (to_rise * rise[f] + to_fall * fall[f])
            for f in range(3)
        ]
        new[0] -= c * ((east[1] - west[1]) + (rise[2] - fall[2]))
        new[1] += d * here[2] - half_step * (east[0] - west[0])
        new[2] -= d * here[1] + half_step * (rise[0] - fall[0])
        for f in range(3):
            store(f, t, new[f])


def kernel(
    nv, nl, x_hbm, wind, depth, out,
    ping, pong, leaving, halo, transit, own, table,
    x_sem, own_sem,
    gs, gr, hs, hr, ts, tr, below, beside, across,
):
    count, _, rows, width = x_hbm.shape
    steps, part = wind.shape[0], wind.shape[3]
    tiles = width // LANES
    v, l = lax.axis_index("vec"), lax.axis_index("lat")
    has = (l > 0, l < nl - 1)
    other = (l - 1, l + 1)
    far = (l - 2, l + 2)
    reaches = (l > 1, l < nl - 2)
    pairs = nl // 2
    odd = lax.rem(l, 2)
    place = l // 2

    def rank(number, wanted):
        return jnp.where(wanted, number, 0) if nl % 2 == 0 else jnp.int32(0)

    relayed = (
        rank(place, (odd == 0) & reaches[0]),
        rank(pairs - 1 - place, (odd == 1) & reaches[1]),
    )
    relaying = (
        rank(place, (odd == 1) & reaches[0]),
        rank(pairs - 1 - place, (odd == 0) & reaches[1]),
    )

    def share(number, s):
        if s == steps - 1:
            return number * count // pairs // 2
        if s == 1:
            return number * (count - 1) // max(pairs - 1, 1)
        return number * count // pairs

    def turn(number, s, k):
        held = share(number, s)
        if s == 0:
            return k >= count - held
        if s == steps - 1:
            return k < held
        return lax.rem(k * (count - held), count) >= count - held

    peers = [lax.rem(v + k, nv) for k in range(1, nv)]
    edge = (0, rows - 1)

    local = [
        pltpu.make_async_copy(x_hbm, ping, x_sem.at[0]),
        pltpu.make_async_copy(wind, own.at[v, :, pl.ds(0, 3)], own_sem.at[0]),
        pltpu.make_async_copy(depth, own.at[v, :, 3], own_sem.at[1]),
    ]
    mate = l + 1 - 2 * odd

    barrier = pltpu.get_barrier_semaphore()

    def greet(semaphore, wanted, device):
        @pl.when(wanted)
        def _():
            pl.semaphore_signal(semaphore, inc=1, device_id=device, device_id_type=MESH)

    pl.semaphore_signal(barrier, inc=1, device_id={"lat": mate}, device_id_type=MESH)
    greet(barrier, reaches[1], {"lat": far[1]})
    for peer in peers:
        greet(barrier, peer > v, {"vec": peer})
    pl.semaphore_wait(barrier, 1 + v + reaches[0].astype(jnp.int32))

    def remote(src, dst, send, recv, target):
        return pltpu.make_async_remote_copy(
            src_ref=src, dst_ref=dst, send_sem=send, recv_sem=recv,
            device_id=target, device_id_type=MESH,
        )

    def lap(s):
        return lax.rem(s, 2)

    def source(side, s, k):
        return x_hbm.at[k, :, pl.ds(edge[side], 1), :] if s == 0 else leaving.at[side, s - 1, k]

    def direct(side, s, k):
        return remote(
            source(side, s, k), halo.at[side, s, k],
            hs.at[side], hr.at[lap(s), k], {"lat": other[side]})

    def detour(side, s, k):
        return remote(
            source(side, s, k), transit.at[s * count + k],
            hs.at[side], tr.at[lap(s), k], {"lat": other[1 - side]})

    def arrival(side, s, k):
        at = transit.at[s * count + k]
        return remote(at, at, hs.at[side], tr.at[lap(s), k], {"lat": other[1 - side]})

    def onward(side, s, k):
        return remote(
            transit.at[s * count + k], halo.at[side, s, k],
            ts.at[0], hr.at[lap(s), k], {"lat": far[side]})

    def send(s, k, which=(True, True)):
        for side in range(2):
            near = odd == 1 - side
            around = turn(relayed[side], s, k)
            if which[0]:
                @pl.when(around)
                def _(side=side):
                    detour(side, s, k).start()
        for side in range(2):
            near = odd == 1 - side
            around = turn(relayed[side], s, k)
            straight = has[side] & jnp.logical_not(around)
            if not which[0]:
                straight &= jnp.logical_not(near)
            if not which[1]:
                straight &= near
            @pl.when(straight)
            def _(side=side):
                direct(side, s, k).start()

    def relay(s, k, due=None):
        for side in range(2):
            @pl.when(turn(relaying[side], s, k) if due is None else due[side])
            def _(side=side):
                arrival(side, s, k).wait_recv()
                onward(side, s, k).start()

    def sent():
        for side in range(2):
            @pl.when(has[side])
            def _(side=side):
                whole = halo.at[side, pl.ds(0, steps)]
                remote(whole, whole, hs.at[side], hr.at[0, 0], {"lat": other[side]}).wait_send()
            for number in range(1, pairs):
                total = sum(share(number, s) for s in range(steps))
                if total == 0:
                    continue

                @pl.when(relaying[side] == number)
                def _(side=side, total=total):
                    whole = transit.at[pl.ds(0, total)]
                    remote(whole, whole, ts.at[0], tr.at[0, 0], {"lat": far[side]}).wait_send()

    def spread(s, n, peer):
        return [
            remote(wind.at[s], own.at[v, s, pl.ds(0, 3)], gs.at[0], gr.at[s], {"vec": peer}),
            remote(depth.at[s], own.at[v, s, 3], gs.at[0], gr.at[s], {"vec": peer}),
        ]

    def gathered(s):
        whole = own.at[pl.ds(0, nv - 1), s]
        return remote(whole, whole, gs.at[0], gr.at[s], {"vec": peers[0]})
    send(0, 0, (True, False))
    for copy in local:
        copy.start()
    greet(below, reaches[0], {"lat": far[0]})
    greet(beside, (odd == 1) & reaches[0], {"lat": mate})
    for peer in peers:
        greet(across, peer < v, {"vec": peer})

    @pl.loop(1, count)
    def _(k):
        send(0, k, (True, False))

    def share_out(s, wanted):
        for n, peer in enumerate(peers):
            @pl.when(wanted(peer))
            def _(s=s, n=n, peer=peer):
                for copy in spread(s, n, peer):
                    copy.start()

    share_out(0, lambda peer: peer < v)

    @pl.when((odd == 1) & reaches[1])
    def _():
        pl.semaphore_wait(below, 1)

    @pl.when((odd == 0) & reaches[0])
    def _():
        pl.semaphore_wait(beside, 1)

    @pl.loop(0, count)
    def _(k):
        send(0, k, (False, True))

    @pl.when(v < nv - 1)
    def _():
        pl.semaphore_wait(across, nv - 1 - v)

    share_out(0, lambda peer: peer > v)
    for s in range(1, steps):
        share_out(s, lambda peer: peer >= 0)

    @pl.when((odd == 0) & reaches[1])
    def _():
        pl.semaphore_wait(below, 1)

    for side in range(2):
        @pl.when(jnp.logical_not(has[side]))
        def _(side=side):
            halo[1 - side, steps, 0] = jnp.zeros((3, 1, width), jnp.float32)

    for k in range(LEAD):
        relay(0, k)
    for copy in local:
        copy.wait()

    def span(t):
        return pl.ds(t * LANES, LANES)

    for s in range(steps):
        gathered(s).wait_recv()
        for t in range(tiles):
            block, offset = divmod(t * LANES, part)
            a, b, d, c = (own[block, s, q, :, pl.ds(offset, LANES)] for q in range(4))
            a, b = half_step * a, half_step * b
            values = (side_weight - a, side_weight + a, side_weight - b, side_weight + b, time_step * d, half_step * c)
            for q, value in enumerate(values):
                table[q, :, span(t)] = value

        final = s == steps - 1
        old = ping if s == 0 else (out, pong)[(steps - s) % 2]
        new = (out, pong)[(steps - 1 - s) % 2]

        @pl.loop(0, count)
        def _(k, s=s, final=final, old=old, new=new):
            ahead = k + LEAD
            later = ahead >= count
            due = []
            for side in range(2):
                now = turn(relaying[side], s, ahead) & jnp.logical_not(later)
                if not final:
                    now |= turn(relaying[side], s + 1, ahead - count) & later
                due.append(now)
            relay(s + later.astype(jnp.int32), jnp.where(later, ahead - count, ahead), due)
            for ends in (1, 2):
                @pl.when(has[0].astype(jnp.int32) + has[1].astype(jnp.int32) == ends)
                def _(ends=ends):
                    both = halo.at[pl.ds(0, ends), s, k]
                    remote(both, both, hs.at[0], hr.at[lap(s), k], {"lat": other[0]}).wait_recv()
            slot = [
                (jnp.where(has[side], s, steps), jnp.where(has[side], k, 0)) for side in range(2)
            ]

            def load(f, t):
                return old[k, f, :, span(t)]

            def store(f, t, value):
                new[k, f, :, span(t)] = value
                if not final:
                    for side in range(2):
                        leaving[side, s, k, f, :, span(t)] = value[edge[side]:edge[side] + 1]

            def beyond(side, f, t):
                value = halo[1 - side, slot[side][0], slot[side][1], f, :, span(t)]
                return jnp.broadcast_to(value, (rows, LANES))

            def coefficient(q, t):
                return table[q, :, span(t)]

            sweep(load, store, beyond, coefficient, tiles)
            if not final:
                send(s + 1, k)

    whole = own.at[pl.ds(0, nv - 1)]
    remote(whole, whole, gs.at[0], gr.at[0], {"vec": peers[0]}).wait_send()
    sent()


def solution(mesh):
    nv, nl = mesh.shape["vec"], mesh.shape["lat"]

    def shards(perturbation, wind_coriolis, depth_field):
        count, _, rows, width = perturbation.shape
        steps, part = wind_coriolis.shape[0], wind_coriolis.shape[3]
        dma = pltpu.SemaphoreType.DMA
        f32 = jnp.float32
        return pl.pallas_call(
            functools.partial(kernel, nv, nl),
            out_shape=jax.ShapeDtypeStruct(perturbation.shape, f32),
            in_specs=[pl.BlockSpec(memory_space=pltpu.HBM)] * 3,
            out_specs=pl.BlockSpec(memory_space=pltpu.VMEM),
            scratch_shapes=[
                pltpu.VMEM((count, 3, rows, width), f32),
                pltpu.VMEM((count, 3, rows, width), f32),
                pltpu.VMEM((2, steps - 1, count, 3, 1, width), f32),
                pltpu.VMEM((2, steps + 1, count, 3, 1, width), f32),
                pltpu.VMEM((steps * count, 3, 1, width), f32),
                pltpu.VMEM((nv, steps, 4, rows, part), f32),
                pltpu.VMEM((6, rows, width), f32),
                dma((1,)), dma((2,)),
                dma((1,)), dma((steps,)), dma((2,)), dma((2, count)), dma((1,)), dma((2, count)),
                pltpu.SemaphoreType.REGULAR, pltpu.SemaphoreType.REGULAR, pltpu.SemaphoreType.REGULAR,
            ],
            compiler_params=pltpu.CompilerParams(
                collective_id=0, has_side_effects=True, vmem_limit_bytes=40 * 1024 * 1024
            ),
        )(*(pltpu.with_memory_space_constraint(a, pltpu.HBM) for a in (perturbation, wind_coriolis, depth_field)))

    placed = (P("vec", None, "lat", None), P(None, None, "lat", "vec"), P(None, "lat", "vec"))
    return jax.shard_map(
        shards, mesh=mesh, in_specs=placed, out_specs=P("vec", None, "lat", None), check_vma=False
    )
```

```python
import functools

import jax
import jax.numpy as jnp
from jax import lax
from jax.experimental import pallas as pl
from jax.experimental.pallas import tpu as pltpu
from jax.sharding import PartitionSpec as P

MESH = pl.DeviceIdType.MESH
LANES = 128
LEAD = 3
time_step = 0.2
viscosity = 0.05
side_weight = time_step * viscosity
half_step = 0.5 * time_step


def sweep(load, store, halo, coefficient, tiles):
    lane = lax.broadcasted_iota(jnp.int32, (8, LANES), 1)
    row = lax.broadcasted_iota(jnp.int32, (8, LANES), 0)
    first_lane, last_lane = lane == 0, lane == LANES - 1
    first_row, last_row = row == 0, row == 7
    known = {}

    def tile(field, t):
        key = (field, t % tiles)
        if key not in known:
            value = load(field, t % tiles)
            known[key] = (value, pltpu.roll(value, LANES - 1, 1), pltpu.roll(value, 1, 1))
        return known[key]

    for t in range(tiles):
        east, west, rise, fall, here = {}, {}, {}, {}, {}
        for f in range(3):
            before, now, after = (tile(f, t + k) for k in (-1, 0, 1))
            here[f] = now[0]
            east[f] = jnp.where(last_lane, after[1], now[1])
            west[f] = jnp.where(first_lane, before[2], now[2])
            rise[f] = jnp.where(last_row, halo(1, f, t), pltpu.roll(now[0], 7, 0))
            fall[f] = jnp.where(first_row, halo(0, f, t), pltpu.roll(now[0], 1, 0))
        to_east, to_west, to_rise, to_fall, d, c = (coefficient(q, t) for q in range(6))
        new = [
            (1.0 - 4.0 * side_weight) * here[f]
            + (to_east * east[f] + to_west * west[f])
            + (to_rise * rise[f] + to_fall * fall[f])
            for f in range(3)
        ]
        new[0] -= c * ((east[1] - west[1]) + (rise[2] - fall[2]))
        new[1] += d * here[2] - half_step * (east[0] - west[0])
        new[2] -= d * here[1] + half_step * (rise[0] - fall[0])
        for f in range(3):
            store(f, t, new[f])


def kernel(
    nv, nl, x_hbm, wind, depth, out,
    ping, pong, leaving, halo, transit, own, table,
    x_sem, own_sem,
    gs, gr, hs, hr, ts, tr, below, beside, across,
):
    count, _, rows, width = x_hbm.shape
    steps, part = wind.shape[0], wind.shape[3]
    tiles = width // LANES
    v, l = lax.axis_index("vec"), lax.axis_index("lat")
    has = (l > 0, l < nl - 1)
    other = (l - 1, l + 1)
    far = (l - 2, l + 2)
    reaches = (l > 1, l < nl - 2)
    pairs = nl // 2
    odd = lax.rem(l, 2)
    place = l // 2

    def rank(number, wanted):
        return jnp.where(wanted, number, 0) if nl % 2 == 0 else jnp.int32(0)

    relayed = (
        rank(place, (odd == 0) & reaches[0]),
        rank(pairs - 1 - place, (odd == 1) & reaches[1]),
    )
    relaying = (
        rank(place, (odd == 1) & reaches[0]),
        rank(pairs - 1 - place, (odd == 0) & reaches[1]),
    )

    def share(number, s):
        if s == steps - 1:
            return number * count // pairs // 2
        if s == 1:
            return number * (count - 1) // max(pairs - 1, 1)
        return number * count // pairs

    def turn(number, s, k):
        held = share(number, s)
        if s == 0:
            return k >= count - held
        if s == steps - 1:
            return k < held
        return lax.rem(k * (count - held), count) >= count - held

    peers = [lax.rem(v + k, nv) for k in range(1, nv)]
    edge = (0, rows - 1)

    local = [
        pltpu.make_async_copy(x_hbm, ping, x_sem.at[0]),
        pltpu.make_async_copy(wind, own.at[v, :, pl.ds(0, 3)], own_sem.at[0]),
        pltpu.make_async_copy(depth, own.at[v, :, 3], own_sem.at[0]),
    ]
    mate = l + 1 - 2 * odd

    barrier = pltpu.get_barrier_semaphore()

    def greet(semaphore, wanted, device):
        @pl.when(wanted)
        def _():
            pl.semaphore_signal(semaphore, inc=1, device_id=device, device_id_type=MESH)

    pl.semaphore_signal(barrier, inc=1, device_id={"lat": mate}, device_id_type=MESH)
    greet(barrier, reaches[1], {"lat": far[1]})
    for peer in peers:
        greet(barrier, peer > v, {"vec": peer})
    pl.semaphore_wait(barrier, 1 + v + reaches[0].astype(jnp.int32))

    def remote(src, dst, send, recv, target):
        return pltpu.make_async_remote_copy(
            src_ref=src, dst_ref=dst, send_sem=send, recv_sem=recv,
            device_id=target, device_id_type=MESH,
        )

    def lap(s):
        return lax.rem(s, 2)

    def source(side, s, k):
        return x_hbm.at[k, :, pl.ds(edge[side], 1), :] if s == 0 else leaving.at[side, s - 1, k]

    def direct(side, s, k):
        return remote(
            source(side, s, k), halo.at[side, s, k],
            hs.at[0], hr.at[lap(s), k], {"lat": other[side]})

    def detour(side, s, k):
        return remote(
            source(side, s, k), transit.at[s * count + k],
            hs.at[0], tr.at[lap(s), k], {"lat": other[1 - side]})

    def arrival(side, s, k):
        at = transit.at[s * count + k]
        return remote(at, at, hs.at[0], tr.at[lap(s), k], {"lat": other[1 - side]})

    def onward(side, s, k):
        return remote(
            transit.at[s * count + k], halo.at[side, s, k],
            ts.at[0], hr.at[lap(s), k], {"lat": far[side]})

    def send(s, k, which=(True, True)):
        for side in range(2):
            near = odd == 1 - side
            around = turn(relayed[side], s, k)
            if which[0]:
                @pl.when(around)
                def _(side=side):
                    detour(side, s, k).start()
        for side in range(2):
            near = odd == 1 - side
            around = turn(relayed[side], s, k)
            straight = has[side] & jnp.logical_not(around)
            if not which[0]:
                straight &= jnp.logical_not(near)
            if not which[1]:
                straight &= near
            @pl.when(straight)
            def _(side=side):
                direct(side, s, k).start()

    def relay(s, k, due=None):
        for side in range(2):
            @pl.when(turn(relaying[side], s, k) if due is None else due[side])
            def _(side=side):
                arrival(side, s, k).wait_recv()
                onward(side, s, k).start()

    def sent():
        for ends in (1, 2):
            @pl.when(has[0].astype(jnp.int32) + has[1].astype(jnp.int32) == ends)
            def _(ends=ends):
                whole = halo.at[pl.ds(0, ends), pl.ds(0, steps)]
                remote(whole, whole, hs.at[0], hr.at[0, 0], {"lat": other[0]}).wait_send()
        for side in range(2):
            for number in range(1, pairs):
                total = sum(share(number, s) for s in range(steps))
                if total == 0:
                    continue

                @pl.when(relaying[side] == number)
                def _(side=side, total=total):
                    whole = transit.at[pl.ds(0, total)]
                    remote(whole, whole, ts.at[0], tr.at[0, 0], {"lat": far[side]}).wait_send()

    def spread(s, n, peer):
        return [
            remote(wind.at[s], own.at[v, s, pl.ds(0, 3)], gs.at[0], gr.at[s], {"vec": peer}),
            remote(depth.at[s], own.at[v, s, 3], gs.at[0], gr.at[s], {"vec": peer}),
        ]

    def gathered(s):
        whole = own.at[pl.ds(0, nv - 1), s]
        return remote(whole, whole, gs.at[0], gr.at[s], {"vec": peers[0]})
    send(0, 0, (True, False))
    for copy in local:
        copy.start()
    greet(below, reaches[0], {"lat": far[0]})
    greet(beside, (odd == 1) & reaches[0], {"lat": mate})
    for peer in peers:
        greet(across, peer < v, {"vec": peer})

    @pl.loop(1, count)
    def _(k):
        send(0, k, (True, False))

    def share_out(s, wanted):
        for n, peer in enumerate(peers):
            @pl.when(wanted(peer))
            def _(s=s, n=n, peer=peer):
                for copy in spread(s, n, peer):
                    copy.start()

    share_out(0, lambda peer: peer < v)

    @pl.when((odd == 1) & reaches[1])
    def _():
        pl.semaphore_wait(below, 1)

    @pl.when((odd == 0) & reaches[0])
    def _():
        pl.semaphore_wait(beside, 1)

    @pl.loop(0, count)
    def _(k):
        send(0, k, (False, True))

    @pl.when(v < nv - 1)
    def _():
        pl.semaphore_wait(across, nv - 1 - v)

    share_out(0, lambda peer: peer > v)
    for s in range(1, steps):
        share_out(s, lambda peer: peer >= 0)

    @pl.when((odd == 0) & reaches[1])
    def _():
        pl.semaphore_wait(below, 1)

    for side in range(2):
        @pl.when(jnp.logical_not(has[side]))
        def _(side=side):
            halo[1 - side, steps, 0] = jnp.zeros((3, 1, width), jnp.float32)

    for k in range(LEAD):
        relay(0, k)
    local[0].wait()
    pltpu.make_async_copy(own.at[v], own.at[v], own_sem.at[0]).wait()

    def span(t):
        return pl.ds(t * LANES, LANES)

    for s in range(steps):
        gathered(s).wait_recv()
        for t in range(tiles):
            block, offset = divmod(t * LANES, part)
            a, b, d, c = (own[block, s, q, :, pl.ds(offset, LANES)] for q in range(4))
            a, b = half_step * a, half_step * b
            values = (side_weight - a, side_weight + a, side_weight - b, side_weight + b, time_step * d, half_step * c)
            for q, value in enumerate(values):
                table[q, :, span(t)] = value

        final = s == steps - 1
        old = ping if s == 0 else (out, pong)[(steps - s) % 2]
        new = (out, pong)[(steps - 1 - s) % 2]

        @pl.loop(0, count)
        def _(k, s=s, final=final, old=old, new=new):
            ahead = k + LEAD
            later = ahead >= count
            due = []
            for side in range(2):
                now = turn(relaying[side], s, ahead) & jnp.logical_not(later)
                if not final:
                    now |= turn(relaying[side], s + 1, ahead - count) & later
                due.append(now)
            relay(s + later.astype(jnp.int32), jnp.where(later, ahead - count, ahead), due)
            for ends in (1, 2):
                @pl.when(has[0].astype(jnp.int32) + has[1].astype(jnp.int32) == ends)
                def _(ends=ends):
                    both = halo.at[pl.ds(0, ends), s, k]
                    remote(both, both, hs.at[0], hr.at[lap(s), k], {"lat": other[0]}).wait_recv()
            slot = [
                (jnp.where(has[side], s, steps), jnp.where(has[side], k, 0)) for side in range(2)
            ]

            def load(f, t):
                return old[k, f, :, span(t)]

            def store(f, t, value):
                new[k, f, :, span(t)] = value
                if not final:
                    for side in range(2):
                        leaving[side, s, k, f, :, span(t)] = value[edge[side]:edge[side] + 1]

            def beyond(side, f, t):
                value = halo[1 - side, slot[side][0], slot[side][1], f, :, span(t)]
                return jnp.broadcast_to(value, (rows, LANES))

            def coefficient(q, t):
                return table[q, :, span(t)]

            sweep(load, store, beyond, coefficient, tiles)
            if not final:
                send(s + 1, k)

    whole = own.at[pl.ds(0, nv - 1)]
    remote(whole, whole, gs.at[0], gr.at[0], {"vec": peers[0]}).wait_send()
    sent()


def solution(mesh):
    nv, nl = mesh.shape["vec"], mesh.shape["lat"]

    def shards(perturbation, wind_coriolis, depth_field):
        count, _, rows, width = perturbation.shape
        steps, part = wind_coriolis.shape[0], wind_coriolis.shape[3]
        dma = pltpu.SemaphoreType.DMA
        f32 = jnp.float32
        return pl.pallas_call(
            functools.partial(kernel, nv, nl),
            out_shape=jax.ShapeDtypeStruct(perturbation.shape, f32),
            in_specs=[pl.BlockSpec(memory_space=pltpu.HBM)] * 3,
            out_specs=pl.BlockSpec(memory_space=pltpu.VMEM),
            scratch_shapes=[
                pltpu.VMEM((count, 3, rows, width), f32),
                pltpu.VMEM((count, 3, rows, width), f32),
                pltpu.VMEM((2, steps - 1, count, 3, 1, width), f32),
                pltpu.VMEM((2, steps + 1, count, 3, 1, width), f32),
                pltpu.VMEM((steps * count, 3, 1, width), f32),
                pltpu.VMEM((nv, steps, 4, rows, part), f32),
                pltpu.VMEM((6, rows, width), f32),
                dma((1,)), dma((1,)),
                dma((1,)), dma((steps,)), dma((1,)), dma((2, count)), dma((1,)), dma((2, count)),
                pltpu.SemaphoreType.REGULAR, pltpu.SemaphoreType.REGULAR, pltpu.SemaphoreType.REGULAR,
            ],
            compiler_params=pltpu.CompilerParams(
                collective_id=0, has_side_effects=True, vmem_limit_bytes=40 * 1024 * 1024
            ),
        )(*(pltpu.with_memory_space_constraint(a, pltpu.HBM) for a in (perturbation, wind_coriolis, depth_field)))

    placed = (P("vec", None, "lat", None), P(None, None, "lat", "vec"), P(None, "lat", "vec"))
    return jax.shard_map(
        shards, mesh=mesh, in_specs=placed, out_specs=P("vec", None, "lat", None), check_vma=False
    )
```
